32 devices in a mesh: dom: 32 (over z, y, x, core).
Axes of the slice: x: 2, y: 2, z: 4, core: 2. Of those that a mesh axis runs over, the one named last changes fastest.
Arguments:
- modal_dofs: float32 [35, 9, 8192], P(None, None, 'dom'), may hold values from -6 to 6
- jacobian: float32 [3, 8192], P(None, 'dom'), may hold values from 0.2 to 0.8
- face_area: float32 [4, 8192], P(None, 'dom'), may hold values from 0.1 to 0.4
- cluster_id: int32 [8192], P('dom'), may hold values from 0 to 1
- target_slot: int32 [8192], P('dom'), may hold values from 0 to 383, as said below
- ghost_slots: int32 [32, 8, 6], P('dom'), may hold values from 0 to 383
- face_neighbours: int32 [4, 12288], P(None, 'dom'), may hold values from 0 to 431, as said below
- stiffness: float32 [3, 35, 35], replicated, may hold values from -1 to 1
- star_matrix: float32 [3, 9, 9], replicated, may hold values from -2 to 2
- face_minus: float32 [4, 35, 35], replicated, may hold values from -1 to 1
- face_plus: float32 [4, 35, 35], replicated, may hold values from -1 to 1
- solver_minus: float32 [4, 9, 9], replicated, may hold values from -2 to 2
- solver_plus: float32 [4, 9, 9], replicated, may hold values from -2 to 2
Outputs:
- updated: float32 [35, 9, 8192], P(None, None, 'dom')
The draws below stay inside these ranges and needn't reach their ends.
Inputs may be any that keep to these rules, and one draw needn't show every extreme that they name: `target_slot`: within the 256 elements of one block the values are distinct. One owner, the same for every block, receives 12 elements from every block. `face_neighbours`: values from 384 on address the ghost table of 48 entries.
All inputs are finite; a program needn't handle non-finite values.
Results may differ from the reference program's by a relative error of at most 0.0003.
Values sent between devices are 32-bit elements; how exact they have to be, the bound alone decides.
A program may use at most 64 MiB of HBM per device.

```python
import math
import jax
import jax.numpy as jnp
from jax import lax

ORDER = 5
MODES = 35
QUANT = 9
NEIGH = 8
E_DEV = 256
CAP = 12
SLOTS = 384
GHOSTS = 6
ELEMS = 8192
N_DOM = 32


def draw_target_slot(key, part):
    slot_total = N_DOM * CAP
    full_owner = jax.random.randint(jax.random.fold_in(key, 11), (), 0, N_DOM)
    block_keys = jax.random.split(jax.random.fold_in(key, 12), N_DOM)

    def one_block(block_key):
        order_key = jax.random.fold_in(block_key, 1)
        assign_key = jax.random.fold_in(block_key, 2)
        ranking = jax.random.permutation(order_key, slot_total).astype(jnp.int32)
        slot_ids = jnp.arange(slot_total, dtype=jnp.int32)
        priority = jnp.where(slot_ids // CAP == full_owner, -1, ranking)
        chosen = jnp.argsort(priority, stable=True)[:E_DEV].astype(jnp.int32)
        return chosen[jax.random.permutation(assign_key, E_DEV)]
    return jax.vmap(one_block)(block_keys).reshape(-1).astype(jnp.int32)


def draw_face_neighbours(key, part):
    total = N_DOM * SLOTS
    local_key = jax.random.fold_in(key, 21)
    ghost_key = jax.random.fold_in(key, 22)
    pick_key = jax.random.fold_in(key, 23)
    local_part = jax.random.randint(local_key, (4, total), 0, SLOTS)
    ghost_part = SLOTS + jax.random.randint(ghost_key, (4, total), 0, NEIGH * GHOSTS)
    remote_face = jax.random.randint(pick_key, (4, total), 0, 8) == 0
    return jnp.where(remote_face, ghost_part, local_part).astype(jnp.int32)


def set_ends(values, stream_key, smallest, top_value):
    shape = values.shape
    place = [jax.random.randint(jax.random.fold_in(stream_key, axis), (), 0, shape[axis]) for axis in range(len(shape))]
    values = values.at[tuple(place)].set(smallest)
    longest = shape.index(max(shape))
    place[longest] = (place[longest] + 1) % shape[longest]
    return values.at[tuple(place)].set(top_value)


def block_scale(key, shape, shards, low, top_value):
    def one(dim, shards_of):
        draws = jax.random.uniform(jax.random.fold_in(jax.random.fold_in(key, 6), dim), (shards_of,), jnp.float32, low / len(shards), top_value / len(shards))
        return jnp.repeat(jnp.exp(draws), shape[dim] // shards_of).reshape((-1,) + (1,) * (len(shape) - dim - 1))

    level = one(*shards[0])
    for cut in shards[1:]:
        level = level * one(*cut)
    return level


def normal_values(key, extent, width, reach, cuts=(), kind=jnp.bfloat16):
    entries = width * jax.random.normal(key, extent, jnp.float32)
    if cuts:
        entries = entries * block_scale(key, extent, cuts, -0.22, 0.18)
    return jnp.clip(entries, -reach, reach).astype(kind)


def setup_inputs(seed: int = 0) -> dict:
    key_list = jax.random.split(jax.random.key(seed), 14)
    modal_dofs = normal_values(key_list[0], (MODES, QUANT, ELEMS), 1.0, 6.0, ((2, 32),), jnp.float32)
    jacobian = jnp.clip(jnp.exp(math.log(0.8) - 1.3862944 * jax.random.uniform(key_list[1], (3, ELEMS), jnp.float32) ** block_scale(key_list[1], (3, ELEMS), ((1, 32),), -0.2, 0.2)), 0.2, 0.8)
    face_area = jnp.clip(jnp.exp(math.log(0.4) - 1.3862944 * jax.random.uniform(key_list[2], (4, ELEMS), jnp.float32) ** block_scale(key_list[2], (4, ELEMS), ((1, 32),), -0.2, 0.2)), 0.1, 0.4)
    cluster_id = set_ends(jax.random.randint(key_list[3], (ELEMS,), 0, 2), jax.random.fold_in(key_list[3], 1), 0, 1).astype(jnp.int32)
    target_slot = draw_target_slot(jax.random.fold_in(key_list[13], 71), 0)
    ghost_slots = set_ends(jax.random.randint(key_list[5], (N_DOM, NEIGH, GHOSTS), 0, SLOTS), jax.random.fold_in(key_list[5], 1), 0, SLOTS - 1).astype(jnp.int32)
    face_neighbours = draw_face_neighbours(jax.random.fold_in(key_list[13], 71), 0)
    stiffness = normal_values(key_list[7], (3, MODES, MODES), MODES ** -0.5, 1.0, (), jnp.float32)
    star_matrix = normal_values(key_list[8], (3, QUANT, QUANT), QUANT ** -0.5, 2.0, (), jnp.float32)
    face_minus = normal_values(key_list[9], (4, MODES, MODES), MODES ** -0.5, 1.0, (), jnp.float32)
    face_plus = normal_values(key_list[10], (4, MODES, MODES), MODES ** -0.5, 1.0, (), jnp.float32)
    solver_minus = normal_values(key_list[11], (4, QUANT, QUANT), QUANT ** -0.5, 2.0, (), jnp.float32)
    solver_plus = normal_values(key_list[12], (4, QUANT, QUANT), QUANT ** -0.5, 2.0, (), jnp.float32)
    return {"modal_dofs": modal_dofs, "jacobian": jacobian, "face_area": face_area, "cluster_id": cluster_id, "target_slot": target_slot, "ghost_slots": ghost_slots, "face_neighbours": face_neighbours, "stiffness": stiffness, "star_matrix": star_matrix, "face_minus": face_minus, "face_plus": face_plus, "solver_minus": solver_minus, "solver_plus": solver_plus}


exact_precision = lax.Precision.HIGHEST
neighbour_steps = (1, -1, 2, -2, 3, -3, 4, -4)


def coefficients(lower_end, upper_end):
    return [(upper_end ** (degree + 1) - lower_end ** (degree + 1)) / math.factorial(degree + 1) for degree in range(ORDER)]


def derive(start_state, scaling, stiffness, star_matrix):
    taylor_terms = [start_state]
    current = start_state
    for degree in range(ORDER - 1):
        rotated = jnp.einsum('cmn,mqs->cnqs', stiffness, current, precision=exact_precision)
        rotated = rotated * scaling[:, None, None, :]
        current = -jnp.einsum('cnqs,cqp->nps', rotated, star_matrix, precision=exact_precision)
        taylor_terms.append(current)
    return taylor_terms


def combine_terms(taylor_terms, factors):
    summed = taylor_terms[0] * factors[0]
    for series_term, factor in zip(taylor_terms[1:], factors[1:]):
        summed = summed + series_term * factor
    return summed


def increment(values, beside, scaling, face_scale, stiffness, star_matrix, face_minus, face_plus, solver_minus, solver_plus):
    volume = jnp.einsum('cnm,mqs->cnqs', stiffness, values, precision=exact_precision) * scaling[:, None, None, :]
    volume = jnp.einsum('cnqs,cqp->nps', volume, star_matrix, precision=exact_precision)
    local_flux = jnp.einsum('fnm,mqs->fnqs', face_minus, values, precision=exact_precision) * face_scale[:, None, None, :]
    local_flux = jnp.einsum('fnqs,fqp->nps', local_flux, solver_minus, precision=exact_precision)
    remote = jnp.einsum('fnm,mqfs->fnqs', face_plus, beside, precision=exact_precision) * face_scale[:, None, None, :]
    remote = jnp.einsum('fnqs,fqp->nps', remote, solver_plus, precision=exact_precision)
    return volume - local_flux - remote


def reference(modal_dofs, jacobian, face_area, cluster_id, target_slot, ghost_slots, face_neighbours, stiffness, star_matrix, face_minus, face_plus, solver_minus, solver_plus):
    slot_total = N_DOM * SLOTS
    element = jnp.arange(ELEMS, dtype=jnp.int32)
    block_id = element // E_DEV
    owner_index = (target_slot // CAP) * SLOTS + block_id * CAP + target_slot % CAP
    owned = jnp.zeros((MODES, QUANT, slot_total), jnp.float32).at[:, :, owner_index].set(modal_dofs)
    owned_jac = jnp.zeros((3, slot_total), jnp.float32).at[:, owner_index].set(jacobian)
    owned_area = jnp.zeros((4, slot_total), jnp.float32).at[:, owner_index].set(face_area)
    weight = jnp.zeros((slot_total,), jnp.float32).at[owner_index].set(1.0 + cluster_id.astype(jnp.float32))
    slot_id = jnp.arange(slot_total, dtype=jnp.int32)
    owner_id = slot_id // SLOTS
    step_table = jnp.array(neighbour_steps, dtype=jnp.int32)
    beyond = jnp.maximum(face_neighbours - SLOTS, 0).astype(jnp.int32)
    neighbour_id = jnp.minimum(beyond // GHOSTS, NEIGH - 1).astype(jnp.int32)
    peer_id = ((owner_id[None, :] - step_table[neighbour_id]) % N_DOM).astype(jnp.int32)
    remote_slot = ghost_slots[peer_id, neighbour_id, beyond % GHOSTS]
    source = jnp.where(face_neighbours < SLOTS, owner_id[None, :] * SLOTS + face_neighbours, peer_id * SLOTS + remote_slot).astype(jnp.int32)
    positions = jnp.arange(N_DOM, dtype=jnp.int32)

    def spread(stacked):
        return jnp.moveaxis(stacked, 0, 2).reshape(MODES, QUANT, slot_total)

    def first_section(position):
        offset = position * SLOTS
        start_state = lax.dynamic_slice_in_dim(owned, offset, SLOTS, 2)
        scaling = lax.dynamic_slice_in_dim(owned_jac, offset, SLOTS, 1)
        taylor_terms = derive(start_state, scaling, stiffness, star_matrix)
        return combine_terms(taylor_terms, coefficients(0.0, 1.0)), combine_terms(taylor_terms, coefficients(1.0, 2.0))

    first_part, later_part = lax.map(first_section, positions)
    first_part = spread(first_part)
    later_part = spread(later_part)

    def update_section(values, current):
        def update_owner(position):
            offset = position * SLOTS
            block_values = lax.dynamic_slice_in_dim(values, offset, SLOTS, 2)
            picked = lax.dynamic_slice_in_dim(source, offset, SLOTS, 1).reshape(-1)
            beside = jnp.take(values, picked, axis=2).reshape(MODES, QUANT, 4, SLOTS)
            scaling = lax.dynamic_slice_in_dim(owned_jac, offset, SLOTS, 1)
            face_scale = lax.dynamic_slice_in_dim(owned_area, offset, SLOTS, 1)
            occupied = (lax.dynamic_slice_in_dim(weight, offset, SLOTS, 0) > 0.5).astype(jnp.float32)
            change = increment(block_values, beside, scaling, face_scale, stiffness, star_matrix, face_minus, face_plus, solver_minus, solver_plus)
            return lax.dynamic_slice_in_dim(current, offset, SLOTS, 2) + occupied * change
        return spread(lax.map(update_owner, positions))

    middle = update_section(first_part, owned)

    def second_section(position):
        offset = position * SLOTS
        start_state = lax.dynamic_slice_in_dim(middle, offset, SLOTS, 2)
        scaling = lax.dynamic_slice_in_dim(owned_jac, offset, SLOTS, 1)
        fresh_part = combine_terms(derive(start_state, scaling, stiffness, star_matrix), coefficients(0.0, 1.0))
        slow_mask = lax.dynamic_slice_in_dim(weight, offset, SLOTS, 0) > 1.5
        return jnp.where(slow_mask[None, None, :], lax.dynamic_slice_in_dim(later_part, offset, SLOTS, 2), fresh_part)

    second = spread(lax.map(second_section, positions))
    final_state = update_section(second, middle)
    return final_state[:, :, owner_index]
```

```python
import functools
import math

import jax
import jax.numpy as jnp
import numpy as np
from jax import lax
from jax.experimental import pallas as pl
from jax.experimental.pallas import tpu as pltpu
from jax.sharding import PartitionSpec as P

ORDER = 5
LANES = 128
SUB = 8
MESH = pl.DeviceIdType.MESH
neighbour_steps = (1, -1, 2, -2, 3, -3, 4, -4)


def coefficients(lower_end, upper_end):
    return [
        (upper_end ** (degree + 1) - lower_end ** (degree + 1)) / math.factorial(degree + 1)
        for degree in range(ORDER)
    ]


def round_up(value, multiple):
    return -(-value // multiple) * multiple


def dot(a, b, dims=((1,), (0,))):
    return lax.dot_general(a, b, (dims, ((), ())), preferred_element_type=jnp.float32)


def halves(x):
    hi = x.astype(jnp.bfloat16)
    lo = (x - hi.astype(jnp.float32)).astype(jnp.bfloat16)
    return hi, lo


def thirds(x):
    hi = x.astype(jnp.bfloat16)
    rest = x - hi.astype(jnp.float32)
    mid = rest.astype(jnp.bfloat16)
    lo = (rest - mid.astype(jnp.float32)).astype(jnp.bfloat16)
    return hi, mid, lo


def triple(x):
    hi, lo = halves(x)
    return jnp.concatenate([hi, lo, hi], axis=1)


def as_bf16(mask):
    return mask.astype(jnp.float32).astype(jnp.bfloat16)


def kernel(
    n,
    extra_at,
    dofs_ref,
    jac_ref,
    area_ref,
    cluster_ref,
    target_ref,
    ghost_ref,
    face_ref,
    spread_mode_ref,
    spread_quant_ref,
    stiff_ref,
    star_ref,
    face_minus_ref,
    face_plus_ref,
    solver_minus_ref,
    solver_plus_ref,
    out_ref,
    staged,
    send_a,
    recv_a,
    send_b,
    recv_b,
    ghost_send,
    ghost_recv,
    state,
    later_ref,
    w_derive,
    w_local,
    w_plus,
    pick_face,
    pick_ghost,
    pick_back,
    ghost_idx,
    face_idx,
    target_idx,
    send_sem,
    recv_sem,
    back_send_sem,
    back_recv_sem,
    ghost_send_sem,
    ghost_recv_sem,
):
    me = lax.axis_index("dom")
    flat, elements = dofs_ref.shape
    width = staged.shape[0]
    slots = state.shape[0]
    cap = slots // n
    beside = len(neighbour_steps)
    ghosts = ghost_ref.shape[1]
    faces = face_ref.shape[0]
    dirs = stiff_ref.shape[0]

    barrier = pltpu.get_barrier_semaphore()

    def greet(d, carry):
        pl.semaphore_signal(barrier, inc=1, device_id=(lax.rem(me + d, n),), device_id_type=MESH)
        return carry

    lax.fori_loop(1, n, greet, 0)

    staged[...] = jnp.zeros_like(staged)
    staged[0:flat, :] = dofs_ref[...]
    staged[extra_at : extra_at + dirs, :] = jac_ref[...]
    staged[extra_at + dirs : extra_at + dirs + faces, :] = area_ref[...]
    staged[extra_at + dirs + faces : extra_at + dirs + faces + 1, :] = 1.0 + cluster_ref[
        ...
    ].astype(jnp.float32)
    scatter = as_bf16(
        lax.broadcasted_iota(jnp.int32, (slots, elements), 0) == target_ref[...]
    )
    hi, mid, lo = thirds(staged[...])
    nt = ((1,), (1,))
    rows = (dot(scatter, lo, nt) + dot(scatter, mid, nt)) + dot(scatter, hi, nt)
    for r in range(n):
        send_a[r] = rows[r * cap : (r + 1) * cap, :]

    pl.semaphore_wait(barrier, n - 1)

    def piece(source, landing, out_sem, in_sem, d):
        peer = lax.rem(me + d, n)
        return pltpu.make_async_remote_copy(
            src_ref=source.at[peer],
            dst_ref=landing.at[me],
            send_sem=out_sem.at[d],
            recv_sem=in_sem.at[d],
            device_id=(peer,),
            device_id_type=MESH,
        )

    def start_all(source, landing, out_sem, in_sem):
        def body(d, carry):
            piece(source, landing, out_sem, in_sem, d).start()
            return carry

        lax.fori_loop(1, n, body, 0)
        landing[me] = source[me]

    def wait_all(source, landing, out_sem, in_sem):
        def body(d, carry):
            piece(source, landing, out_sem, in_sem, d).wait()
            return carry

        lax.fori_loop(1, n, body, 0)

    start_all(send_a, recv_a, send_sem, recv_sem)

    target_idx[...] = jnp.zeros_like(target_idx)
    target_idx[0:1, :] = target_ref[...].astype(jnp.float32)
    target_col = jnp.transpose(target_idx[...])[:, 0:1].astype(jnp.int32)
    pick_back[...] = as_bf16(
        lax.broadcasted_iota(jnp.int32, (elements, slots), 1) == target_col
    )
    ghost_idx[...] = jnp.full_like(ghost_idx, -1.0)
    ghost_idx[:, 0:ghosts] = ghost_ref[...].astype(jnp.float32)
    ghost_cols = jnp.transpose(ghost_idx[...])[0:SUB, :].astype(jnp.int32)
    place = lax.broadcasted_iota(jnp.int32, (SUB, slots), 1)
    for b in range(beside):
        pick_ghost[b] = (place == ghost_cols[:, b : b + 1]).astype(jnp.float32)
    face_idx[...] = jnp.zeros_like(face_idx)
    listed = face_ref[...]
    shift = jnp.zeros_like(listed)
    for b in range(1, beside):
        shift = shift + (listed >= slots + b * ghosts).astype(jnp.int32) * (SUB - ghosts)
    face_idx[0:faces, :] = (listed + shift).astype(jnp.float32)
    face_cols = jnp.transpose(face_idx[...]).astype(jnp.int32)
    reach = pick_face.shape[2]
    for f in range(faces):
        pick_face[f] = as_bf16(
            lax.broadcasted_iota(jnp.int32, (slots, reach), 1) == face_cols[:, f : f + 1]
        )

    spread_mode = spread_mode_ref[...]
    spread_quant = spread_quant_ref[...]

    def expand(table, spread, transposed):
        hi, lo = halves(table)
        dims = ((1,), (1,)) if transposed else ((1,), (0,))
        left = dot(spread, hi, dims) + dot(spread, lo, dims)
        hi, lo = halves(left)
        return dot(hi, spread, nt) + dot(lo, spread, nt)

    def fill(ref, column, modes, quants):
        hi, lo = halves(modes * quants)
        at = slice(column * width, (column + 1) * width)
        ref[0:width, at] = hi
        ref[width : 2 * width, at] = hi
        ref[2 * width : 3 * width, at] = lo

    for c in range(dirs):
        quants = expand(star_ref[c], spread_quant, False)
        fill(w_derive, c, expand(stiff_ref[c], spread_mode, False), -quants)
        fill(w_local, c, expand(stiff_ref[c], spread_mode, True), quants)
    for f in range(faces):
        quants = expand(solver_minus_ref[f], spread_quant, False)
        fill(w_local, dirs + f, expand(face_minus_ref[f], spread_mode, True), -quants)
        quants = expand(solver_plus_ref[f], spread_quant, False)
        fill(w_plus.at[f], 0, expand(face_plus_ref[f], spread_mode, True), -quants)

    wait_all(send_a, recv_a, send_sem, recv_sem)
    for r in range(n):
        state[r * cap : (r + 1) * cap, :] = recv_a[r]

    start = state[...]
    scale = [start[:, extra_at + i : extra_at + i + 1] for i in range(dirs + faces)]
    weight = start[:, extra_at + dirs + faces : extra_at + dirs + faces + 1]
    occupied = (weight > 0.5).astype(jnp.float32)
    slow = (weight > 1.5).astype(jnp.float32)

    def derive(current):
        wide = dot(triple(current), w_derive[...])
        total = scale[0] * wide[:, 0:width]
        for c in range(1, dirs):
            total = total + scale[c] * wide[:, c * width : (c + 1) * width]
        return total

    def advance(values, current, step):
        hi, lo = halves(values)
        both = jnp.concatenate([hi, lo], axis=1)
        for b in range(beside):
            out = dot(pick_ghost[b].astype(jnp.bfloat16), both)
            ghost_send[step, b] = out[:, 0:width] + out[:, width:]
        copies = []
        for b, offset in enumerate(neighbour_steps):
            copy = pltpu.make_async_remote_copy(
                src_ref=ghost_send.at[step, b],
                dst_ref=ghost_recv.at[step, b],
                send_sem=ghost_send_sem.at[step, b],
                recv_sem=ghost_recv_sem.at[step, b],
                device_id=(lax.rem(me + offset + n, n),),
                device_id_type=MESH,
            )
            copy.start()
            copies.append(copy)
        wide = dot(jnp.concatenate([hi, lo, hi], axis=1), w_local[...])
        change = scale[0] * wide[:, 0:width]
        for i in range(1, dirs + faces):
            change = change + scale[i] * wide[:, i * width : (i + 1) * width]
        for copy in copies:
            copy.wait()
        arrived = jnp.concatenate([ghost_recv[step, b] for b in range(beside)], axis=0)
        ghost_hi, ghost_lo = halves(arrived)
        table = jnp.concatenate(
            [both, jnp.concatenate([ghost_hi, ghost_lo], axis=1)], axis=0
        )
        for f in range(faces):
            picked = dot(pick_face[f], table).astype(jnp.bfloat16)
            picked = jnp.concatenate([picked, picked[:, 0:width]], axis=1)
            change = change + scale[dirs + f] * dot(picked, w_plus[f])
        return current + occupied * change

    near, far = coefficients(0.0, 1.0), coefficients(1.0, 2.0)
    first = start * near[0]
    later = start * far[0]
    current = start
    for k in range(1, ORDER):
        current = derive(current)
        first = first + current * near[k]
        later = later + current * far[k]
    later_ref[...] = later
    middle = advance(first, start, 0)
    fresh = middle * near[0]
    current = middle
    for k in range(1, ORDER):
        current = derive(current)
        fresh = fresh + current * near[k]
    second = jnp.where(slow > 0.5, later_ref[...], fresh)
    final = advance(second, middle, 1)
    for r in range(n):
        send_b[r] = final[r * cap : (r + 1) * cap, :]
    start_all(send_b, recv_b, back_send_sem, back_recv_sem)
    wait_all(send_b, recv_b, back_send_sem, back_recv_sem)
    for r in range(n):
        state[r * cap : (r + 1) * cap, :] = recv_b[r]
    hi, mid, lo = thirds(state[...])
    back = pick_back[...]
    home = (dot(back, lo) + dot(back, mid)) + dot(back, hi)
    out_ref[...] = jnp.transpose(home)[0:flat, :]


def local(
    n,
    modal_dofs,
    jacobian,
    face_area,
    cluster_id,
    target_slot,
    ghost_slots,
    face_neighbours,
    stiffness,
    star_matrix,
    face_minus,
    face_plus,
    solver_minus,
    solver_plus,
):
    modes, quants, elements = modal_dofs.shape
    flat = modes * quants
    slots = face_neighbours.shape[1]
    faces, dirs = face_area.shape[0], jacobian.shape[0]
    cap = slots // n
    beside, ghosts = ghost_slots.shape[1:]
    extra_at = round_up(flat, SUB)
    width = round_up(extra_at + dirs + faces + 1, LANES)
    feature = np.arange(width)
    live = feature < flat
    spread_mode = (feature[:, None] // quants == np.arange(modes)[None, :]) & live[:, None]
    spread_quant = (feature[:, None] % quants == np.arange(quants)[None, :]) & live[:, None]
    vmem = pl.BlockSpec(memory_space=pltpu.VMEM)
    f32, bf16 = jnp.float32, jnp.bfloat16
    dma = pltpu.SemaphoreType.DMA
    args = (
        modal_dofs.reshape(flat, elements),
        jacobian,
        face_area,
        cluster_id.reshape(1, elements),
        target_slot.reshape(1, elements),
        ghost_slots.reshape(beside, ghosts),
        face_neighbours,
        jnp.asarray(spread_mode, bf16),
        jnp.asarray(spread_quant, bf16),
        stiffness,
        star_matrix,
        face_minus,
        face_plus,
        solver_minus,
        solver_plus,
    )
    out = pl.pallas_call(
        functools.partial(kernel, n, extra_at),
        out_shape=jax.ShapeDtypeStruct((flat, elements), f32),
        in_specs=[vmem] * len(args),
        out_specs=vmem,
        scratch_shapes=[
            pltpu.VMEM((width, elements), f32),
            pltpu.VMEM((n, cap, width), f32),
            pltpu.VMEM((n, cap, width), f32),
            pltpu.VMEM((n, cap, width), f32),
            pltpu.VMEM((n, cap, width), f32),
            pltpu.VMEM((2, beside, SUB, width), f32),
            pltpu.VMEM((2, beside, SUB, width), f32),
            pltpu.VMEM((slots, width), f32),
            pltpu.VMEM((slots, width), f32),
            pltpu.VMEM((3 * width, dirs * width), bf16),
            pltpu.VMEM((3 * width, (dirs + faces) * width), bf16),
            pltpu.VMEM((faces, 3 * width, width), bf16),
            pltpu.VMEM((faces, slots, slots + beside * SUB), bf16),
            pltpu.VMEM((beside, SUB, slots), f32),
            pltpu.VMEM((elements, slots), bf16),
            pltpu.VMEM((beside, LANES), f32),
            pltpu.VMEM((SUB, slots), f32),
            pltpu.VMEM((SUB, elements), f32),
            dma((n,)),
            dma((n,)),
            dma((n,)),
            dma((n,)),
            dma((2, beside)),
            dma((2, beside)),
        ],
        compiler_params=pltpu.CompilerParams(
            collective_id=0, has_side_effects=True, vmem_limit_bytes=56 * 2**20
        ),
    )(*args)
    return out.reshape(modes, quants, elements)


def solution(mesh):
    placed = (
        P(None, None, "dom"),
        P(None, "dom"),
        P(None, "dom"),
        P("dom"),
        P("dom"),
        P("dom", None, None),
        P(None, "dom"),
        P(),
        P(),
        P(),
        P(),
        P(),
        P(),
    )
    return jax.shard_map(
        functools.partial(local, mesh.shape["dom"]),
        mesh=mesh,
        in_specs=placed,
        out_specs=P(None, None, "dom"),
        check_vma=False,
    )
```

```python
import functools
import math

import jax
import jax.numpy as jnp
import numpy as np
from jax import lax
from jax.experimental import pallas as pl
from jax.experimental.pallas import tpu as pltpu
from jax.sharding import PartitionSpec as P

ORDER = 5
LANES = 128
SUB = 8
MESH = pl.DeviceIdType.MESH
neighbour_steps = (1, -1, 2, -2, 3, -3, 4, -4)


def coefficients(lower_end, upper_end):
    return [
        (upper_end ** (degree + 1) - lower_end ** (degree + 1)) / math.factorial(degree + 1)
        for degree in range(ORDER)
    ]


def round_up(value, multiple):
    return -(-value // multiple) * multiple


def dot(a, b, dims=((1,), (0,))):
    return lax.dot_general(a, b, (dims, ((), ())), preferred_element_type=jnp.float32)


def halves(x):
    hi = x.astype(jnp.bfloat16)
    lo = (x - hi.astype(jnp.float32)).astype(jnp.bfloat16)
    return hi, lo


def thirds(x):
    hi = x.astype(jnp.bfloat16)
    rest = x - hi.astype(jnp.float32)
    mid = rest.astype(jnp.bfloat16)
    lo = (rest - mid.astype(jnp.float32)).astype(jnp.bfloat16)
    return hi, mid, lo


def triple(x):
    hi, lo = halves(x)
    return jnp.concatenate([hi, lo, hi], axis=1)


def as_bf16(mask):
    return mask.astype(jnp.float32).astype(jnp.bfloat16)


def kernel(
    n,
    extra_at,
    dofs_ref,
    jac_ref,
    area_ref,
    cluster_ref,
    target_ref,
    ghost_ref,
    face_ref,
    spread_mode_ref,
    spread_quant_ref,
    stiff_ref,
    star_ref,
    face_minus_ref,
    face_plus_ref,
    solver_minus_ref,
    solver_plus_ref,
    out_ref,
    staged,
    send_a,
    recv_a,
    send_b,
    recv_b,
    ghost_send,
    ghost_recv,
    state,
    later_ref,
    w_derive,
    w_local,
    w_plus,
    pick_face,
    pick_ghost,
    pick_back,
    ghost_idx,
    face_idx,
    target_idx,
    send_sem,
    recv_sem,
    back_send_sem,
    back_recv_sem,
    ghost_send_sem,
    ghost_recv_sem,
):
    me = lax.axis_index("dom")
    quants, modes, elements = dofs_ref.shape
    pitch = extra_at // quants
    width = staged.shape[0]
    slots = state.shape[0]
    cap = slots // n
    beside = len(neighbour_steps)
    ghosts = ghost_ref.shape[0]
    faces = face_ref.shape[0]
    dirs = stiff_ref.shape[0]

    barrier = pltpu.get_barrier_semaphore()

    def greet(d, carry):
        pl.semaphore_signal(barrier, inc=1, device_id=(lax.rem(me + d, n),), device_id_type=MESH)
        return carry

    lax.fori_loop(1, n, greet, 0)

    staged[...] = jnp.zeros_like(staged)
    for q in range(quants):
        staged[q * pitch : q * pitch + modes, :] = dofs_ref[q]
    staged[extra_at : extra_at + dirs, :] = jac_ref[...]
    staged[extra_at + dirs : extra_at + dirs + faces, :] = area_ref[...]
    staged[extra_at + dirs + faces : extra_at + dirs + faces + 1, :] = 1.0 + cluster_ref[
        ...
    ].astype(jnp.float32)
    scatter = as_bf16(
        lax.broadcasted_iota(jnp.int32, (slots, elements), 0) == target_ref[...]
    )
    hi, mid, lo = thirds(staged[...])
    nt = ((1,), (1,))
    rows = (dot(scatter, lo, nt) + dot(scatter, mid, nt)) + dot(scatter, hi, nt)
    for r in range(n):
        send_a[r] = rows[r * cap : (r + 1) * cap, :]

    pl.semaphore_wait(barrier, n - 1)

    def piece(source, landing, out_sem, in_sem, d):
        peer = lax.rem(me + d, n)
        return pltpu.make_async_remote_copy(
            src_ref=source.at[peer],
            dst_ref=landing.at[me],
            send_sem=out_sem.at[d],
            recv_sem=in_sem.at[d],
            device_id=(peer,),
            device_id_type=MESH,
        )

    def start_all(source, landing, out_sem, in_sem):
        def body(d, carry):
            piece(source, landing, out_sem, in_sem, d).start()
            return carry

        lax.fori_loop(1, n, body, 0)
        landing[me] = source[me]

    def wait_all(source, landing, out_sem, in_sem):
        def body(d, carry):
            piece(source, landing, out_sem, in_sem, d).wait()
            return carry

        lax.fori_loop(1, n, body, 0)

    start_all(send_a, recv_a, send_sem, recv_sem)

    target_idx[...] = jnp.zeros_like(target_idx)
    target_idx[0:1, :] = target_ref[...].astype(jnp.float32)
    target_col = jnp.transpose(target_idx[...])[:, 0:1].astype(jnp.int32)
    pick_back[...] = as_bf16(
        lax.broadcasted_iota(jnp.int32, (elements, slots), 1) == target_col
    )
    ghost_idx[...] = jnp.full_like(ghost_idx, -1)
    for i in range(ghosts):
        ghost_idx[i : i + 1, :] = ghost_ref[i]
    ghost_cols = ghost_idx[...]
    place = lax.broadcasted_iota(jnp.int32, (SUB, slots), 1)
    for b in range(beside):
        pick_ghost[b] = (place == ghost_cols[:, b : b + 1]).astype(jnp.float32)
    face_idx[...] = jnp.zeros_like(face_idx)
    listed = face_ref[...]
    shift = jnp.zeros_like(listed)
    for b in range(1, beside):
        shift = shift + (listed >= slots + b * ghosts).astype(jnp.int32) * (SUB - ghosts)
    face_idx[0:faces, :] = (listed + shift).astype(jnp.float32)
    face_cols = jnp.transpose(face_idx[...]).astype(jnp.int32)
    reach = pick_face.shape[2]
    for f in range(faces):
        pick_face[f] = as_bf16(
            lax.broadcasted_iota(jnp.int32, (slots, reach), 1) == face_cols[:, f : f + 1]
        )

    spread_mode = spread_mode_ref[...]
    spread_quant = spread_quant_ref[...]

    def expand(table, spread, transposed):
        hi, lo = halves(table)
        dims = ((1,), (1,)) if transposed else ((1,), (0,))
        left = dot(spread, hi, dims) + dot(spread, lo, dims)
        hi, lo = halves(left)
        return dot(hi, spread, nt) + dot(lo, spread, nt)

    def fill(ref, column, mode_part, quant_part):
        hi, lo = halves(mode_part * quant_part)
        at = slice(column * width, (column + 1) * width)
        ref[0:width, at] = hi
        ref[width : 2 * width, at] = hi
        ref[2 * width : 3 * width, at] = lo

    for c in range(dirs):
        solver = expand(star_ref[:, c, :], spread_quant, False)
        fill(w_derive, c, expand(stiff_ref[c], spread_mode, False), -solver)
        fill(w_local, c, expand(stiff_ref[c], spread_mode, True), solver)
    for f in range(faces):
        solver = expand(solver_minus_ref[:, f, :], spread_quant, False)
        fill(w_local, dirs + f, expand(face_minus_ref[:, f, :], spread_mode, True), -solver)
        solver = expand(solver_plus_ref[:, f, :], spread_quant, False)
        fill(w_plus.at[f], 0, expand(face_plus_ref[:, f, :], spread_mode, True), -solver)

    wait_all(send_a, recv_a, send_sem, recv_sem)
    for r in range(n):
        state[r * cap : (r + 1) * cap, :] = recv_a[r]

    start = state[...]
    scale = [start[:, extra_at + i : extra_at + i + 1] for i in range(dirs + faces)]
    weight = start[:, extra_at + dirs + faces : extra_at + dirs + faces + 1]
    occupied = (weight > 0.5).astype(jnp.float32)
    slow = (weight > 1.5).astype(jnp.float32)

    def derive(current):
        wide = dot(triple(current), w_derive[...])
        total = scale[0] * wide[:, 0:width]
        for c in range(1, dirs):
            total = total + scale[c] * wide[:, c * width : (c + 1) * width]
        return total

    def advance(values, current, step):
        hi, lo = halves(values)
        both = jnp.concatenate([hi, lo], axis=1)
        for b in range(beside):
            out = dot(pick_ghost[b].astype(jnp.bfloat16), both)
            ghost_send[step, b] = out[:, 0:width] + out[:, width:]
        copies = []
        for b, offset in enumerate(neighbour_steps):
            copy = pltpu.make_async_remote_copy(
                src_ref=ghost_send.at[step, b],
                dst_ref=ghost_recv.at[step, b],
                send_sem=ghost_send_sem.at[step, b],
                recv_sem=ghost_recv_sem.at[step, b],
                device_id=(lax.rem(me + offset + n, n),),
                device_id_type=MESH,
            )
            copy.start()
            copies.append(copy)
        wide = dot(jnp.concatenate([hi, lo, hi], axis=1), w_local[...])
        change = scale[0] * wide[:, 0:width]
        for i in range(1, dirs + faces):
            change = change + scale[i] * wide[:, i * width : (i + 1) * width]
        for copy in copies:
            copy.wait()
        arrived = jnp.concatenate([ghost_recv[step, b] for b in range(beside)], axis=0)
        ghost_hi, ghost_lo = halves(arrived)
        table = jnp.concatenate(
            [both, jnp.concatenate([ghost_hi, ghost_lo], axis=1)], axis=0
        )
        for f in range(faces):
            picked = dot(pick_face[f], table).astype(jnp.bfloat16)
            picked = jnp.concatenate([picked, picked[:, 0:width]], axis=1)
            change = change + scale[dirs + f] * dot(picked, w_plus[f])
        return current + occupied * change

    near, far = coefficients(0.0, 1.0), coefficients(1.0, 2.0)
    first = start * near[0]
    later = start * far[0]
    current = start
    for k in range(1, ORDER):
        current = derive(current)
        first = first + current * near[k]
        later = later + current * far[k]
    later_ref[...] = later
    middle = advance(first, start, 0)
    fresh = middle * near[0]
    current = middle
    for k in range(1, ORDER):
        current = derive(current)
        fresh = fresh + current * near[k]
    second = jnp.where(slow > 0.5, later_ref[...], fresh)
    final = advance(second, middle, 1)
    for r in range(n):
        send_b[r] = final[r * cap : (r + 1) * cap, :]
    start_all(send_b, recv_b, back_send_sem, back_recv_sem)
    wait_all(send_b, recv_b, back_send_sem, back_recv_sem)
    for r in range(n):
        state[r * cap : (r + 1) * cap, :] = recv_b[r]
    hi, mid, lo = thirds(state[...])
    back = pick_back[...]
    home = (dot(back, lo) + dot(back, mid)) + dot(back, hi)
    home = jnp.transpose(home)
    for q in range(quants):
        out_ref[q] = home[q * pitch : q * pitch + modes, :]


def local(
    n,
    modal_dofs,
    jacobian,
    face_area,
    cluster_id,
    target_slot,
    ghost_slots,
    face_neighbours,
    stiffness,
    star_matrix,
    face_minus,
    face_plus,
    solver_minus,
    solver_plus,
):
    modes, quants, elements = modal_dofs.shape
    pitch = round_up(modes, SUB)
    slots = face_neighbours.shape[1]
    faces, dirs = face_area.shape[0], jacobian.shape[0]
    cap = slots // n
    beside, ghosts = ghost_slots.shape[1:]
    extra_at = quants * pitch
    width = round_up(extra_at + dirs + faces + 1, LANES)
    feature = np.arange(width)
    live = (feature < extra_at) & (feature % pitch < modes)
    spread_mode = (feature[:, None] % pitch == np.arange(modes)[None, :]) & live[:, None]
    spread_quant = (feature[:, None] // pitch == np.arange(quants)[None, :]) & live[:, None]
    vmem = pl.BlockSpec(memory_space=pltpu.VMEM)
    f32, bf16 = jnp.float32, jnp.bfloat16
    dma = pltpu.SemaphoreType.DMA
    args = (
        jnp.transpose(modal_dofs, (1, 0, 2)),
        jacobian,
        face_area,
        cluster_id.reshape(1, elements),
        target_slot.reshape(1, elements),
        jnp.transpose(ghost_slots, (2, 0, 1)),
        face_neighbours,
        jnp.asarray(spread_mode, bf16),
        jnp.asarray(spread_quant, bf16),
        stiffness,
        jnp.transpose(star_matrix, (1, 0, 2)),
        jnp.transpose(face_minus, (1, 0, 2)),
        jnp.transpose(face_plus, (1, 0, 2)),
        jnp.transpose(solver_minus, (1, 0, 2)),
        jnp.transpose(solver_plus, (1, 0, 2)),
    )
    out = pl.pallas_call(
        functools.partial(kernel, n, extra_at),
        out_shape=jax.ShapeDtypeStruct((quants, modes, elements), f32),
        in_specs=[vmem] * len(args),
        out_specs=vmem,
        scratch_shapes=[
            pltpu.VMEM((width, elements), f32),
            pltpu.VMEM((n, cap, width), f32),
            pltpu.VMEM((n, cap, width), f32),
            pltpu.VMEM((n, cap, width), f32),
            pltpu.VMEM((n, cap, width), f32),
            pltpu.VMEM((2, beside, SUB, width), f32),
            pltpu.VMEM((2, beside, SUB, width), f32),
            pltpu.VMEM((slots, width), f32),
            pltpu.VMEM((slots, width), f32),
            pltpu.VMEM((3 * width, dirs * width), bf16),
            pltpu.VMEM((3 * width, (dirs + faces) * width), bf16),
            pltpu.VMEM((faces, 3 * width, width), bf16),
            pltpu.VMEM((faces, slots, slots + beside * SUB), bf16),
            pltpu.VMEM((beside, SUB, slots), f32),
            pltpu.VMEM((elements, slots), bf16),
            pltpu.VMEM((SUB, beside), jnp.int32),
            pltpu.VMEM((SUB, slots), f32),
            pltpu.VMEM((SUB, elements), f32),
            dma((n,)),
            dma((n,)),
            dma((n,)),
            dma((n,)),
            dma((2, beside)),
            dma((2, beside)),
        ],
        compiler_params=pltpu.CompilerParams(
            collective_id=0, has_side_effects=True, vmem_limit_bytes=56 * 2**20
        ),
    )(*args)
    return jnp.transpose(out, (1, 0, 2))


def solution(mesh):
    placed = (
        P(None, None, "dom"),
        P(None, "dom"),
        P(None, "dom"),
        P("dom"),
        P("dom"),
        P("dom", None, None),
        P(None, "dom"),
        P(),
        P(),
        P(),
        P(),
        P(),
        P(),
    )
    return jax.shard_map(
        functools.partial(local, mesh.shape["dom"]),
        mesh=mesh,
        in_specs=placed,
        out_specs=P(None, None, "dom"),
        check_vma=False,
    )
```

```python
import functools
import math

import jax
import jax.numpy as jnp
import numpy as np
from jax import lax
from jax.experimental import pallas as pl
from jax.experimental.pallas import tpu as pltpu
from jax.sharding import PartitionSpec as P

ORDER = 5
LANES = 128
SUB = 8
MESH = pl.DeviceIdType.MESH
neighbour_steps = (1, -1, 2, -2, 3, -3, 4, -4)


def coefficients(lower_end, upper_end):
    return [
        (upper_end ** (degree + 1) - lower_end ** (degree + 1)) / math.factorial(degree + 1)
        for degree in range(ORDER)
    ]


def round_up(value, multiple):
    return -(-value // multiple) * multiple


def dot(a, b, dims=((1,), (0,))):
    return lax.dot_general(a, b, (dims, ((), ())), preferred_element_type=jnp.float32)


def halves(x):
    hi = x.astype(jnp.bfloat16)
    lo = (x - hi.astype(jnp.float32)).astype(jnp.bfloat16)
    return hi, lo


def thirds(x):
    hi = x.astype(jnp.bfloat16)
    rest = x - hi.astype(jnp.float32)
    mid = rest.astype(jnp.bfloat16)
    lo = (rest - mid.astype(jnp.float32)).astype(jnp.bfloat16)
    return hi, mid, lo


def triple(x):
    hi, lo = halves(x)
    return jnp.concatenate([hi, lo, hi], axis=1)


def as_bf16(mask):
    return mask.astype(jnp.float32).astype(jnp.bfloat16)


def kernel(
    n,
    dofs_ref,
    jac_ref,
    area_ref,
    cluster_ref,
    target_ref,
    ghost_ref,
    face_ref,
    spread_mode_ref,
    spread_quant_ref,
    stiff_ref,
    star_ref,
    face_minus_ref,
    face_plus_ref,
    solver_minus_ref,
    solver_plus_ref,
    out_ref,
    staged,
    send_a,
    recv_a,
    send_b,
    recv_b,
    ghost_send,
    ghost_recv,
    state,
    extra_rows,
    first_ref,
    later_ref,
    w_derive,
    w_local,
    w_plus,
    pick_face,
    pick_ghost,
    pick_back,
    ghost_idx,
    face_idx,
    target_idx,
    extras,
    send_sem,
    recv_sem,
    back_send_sem,
    back_recv_sem,
    ghost_send_sem,
    ghost_recv_sem,
):
    me = lax.axis_index("dom")
    quants, modes, elements = dofs_ref.shape
    flat = quants * modes
    width = state.shape[1]
    whole_tiles = width // LANES - 1
    slots = state.shape[0]
    cap = slots // n
    paired = -(-cap // 2)
    half = n // 2
    half_rows = half * cap
    near_base = half * (me // half)
    far_base = half - near_base
    turn = far_base * cap
    beside = len(neighbour_steps)
    ghosts = ghost_ref.shape[0]
    faces = face_ref.shape[0]
    dirs = stiff_ref.shape[0]

    barrier = pltpu.get_barrier_semaphore()

    def greet(d, carry):
        pl.semaphore_signal(barrier, inc=1, device_id=(lax.rem(me + d, n),), device_id_type=MESH)
        return carry

    lax.fori_loop(1, n, greet, 0)

    def row_of(slot):
        moved = slot - turn
        return moved + slots * (moved < 0).astype(jnp.int32)

    own_lanes = lax.broadcasted_iota(jnp.int32, (cap, LANES), 0) == (
        lax.broadcasted_iota(jnp.int32, (cap, LANES), 1) // SUB
    )

    def pack(values, buffer, owners):
        side = values[:, whole_tiles * LANES : width]
        turned = pltpu.roll(side, LANES // 2, 1)
        for j, owner in enumerate(owners):
            lo = j * cap
            for t in range(whole_tiles):
                buffer[owner, t * cap : (t + 1) * cap, :] = values[
                    lo : lo + cap, t * LANES : (t + 1) * LANES
                ]
            at = whole_tiles * cap
            upper = cap - paired
            if upper < paired:
                buffer[owner, at : at + paired, :] = side[lo : lo + paired]
            buffer[owner, at : at + upper, :] = (
                side[lo : lo + upper] + turned[lo + paired : lo + cap]
            )

    def unpack(buffer, part):
        first_owner = far_base if part == 0 else near_base
        for j in range(half):
            owner = first_owner + j
            lo = part * half_rows + j * cap
            for t in range(whole_tiles):
                state[lo : lo + cap, t * LANES : (t + 1) * LANES] = buffer[
                    owner, t * cap : (t + 1) * cap, :
                ]
            at = whole_tiles * cap
            side = buffer[owner, at : at + paired, :]
            turned = pltpu.roll(side, LANES // 2, 1)
            state[lo : lo + paired, whole_tiles * LANES : width] = side
            state[lo + paired : lo + cap, whole_tiles * LANES : width] = turned[0 : cap - paired]
        values = state[part * half_rows : (part + 1) * half_rows, :]
        lane = lax.broadcasted_iota(jnp.int32, values.shape, 1)
        return jnp.where(lane < flat, values, 0.0)

    staged[...] = jnp.zeros_like(staged)
    for q in range(quants):
        staged[q * modes : (q + 1) * modes, :] = dofs_ref[q]
    extras[...] = jnp.zeros_like(extras)
    extras[0:dirs, :] = jac_ref[...]
    extras[dirs : dirs + faces, :] = area_ref[...]
    extras[dirs + faces : dirs + faces + 1, :] = 1.0 + cluster_ref[...].astype(jnp.float32)
    staged[width : width + LANES, :] = jnp.concatenate([extras[...]] * (LANES // SUB), axis=0)
    scatter = as_bf16(
        lax.broadcasted_iota(jnp.int32, (slots, elements), 0) == target_ref[...]
    )
    hi, mid, lo = thirds(staged[...])
    nt = ((1,), (1,))
    rows = (dot(scatter, lo, nt) + dot(scatter, mid, nt)) + dot(scatter, hi, nt)
    pack(rows[:, 0:width], send_a, range(n))
    extra_row = whole_tiles * cap + paired
    for o in range(n):
        listed = jnp.where(own_lanes, rows[o * cap : (o + 1) * cap, width : width + LANES], 0.0)
        send_a[o, extra_row : extra_row + 1, :] = jnp.sum(listed, axis=0, keepdims=True)

    pl.semaphore_wait(barrier, n - 1)

    def outgoing(source, landing, out_sem, in_sem, peer):
        return pltpu.make_async_remote_copy(
            src_ref=source.at[peer],
            dst_ref=landing.at[me],
            send_sem=out_sem.at[peer],
            recv_sem=in_sem.at[me],
            device_id=(peer,),
            device_id_type=MESH,
        )

    def incoming(source, landing, out_sem, in_sem, peer):
        return pltpu.make_async_remote_copy(
            src_ref=source.at[peer],
            dst_ref=landing.at[peer],
            send_sem=out_sem.at[peer],
            recv_sem=in_sem.at[peer],
            device_id=(peer,),
            device_id_type=MESH,
        )

    mine = me - near_base

    def far_peer(j):
        return far_base + lax.rem(mine + j, half)

    def near_peer(j):
        return near_base + lax.rem(mine + j, half)

    def each(peer_of, first, action, *refs):
        def body(j, carry):
            action(*refs, peer_of(j))
            return carry

        lax.fori_loop(first, half, body, 0)

    def start(*refs):
        outgoing(*refs).start()

    def wait_in(*refs):
        incoming(*refs).wait_recv()

    def wait_out(*refs):
        outgoing(*refs).wait_send()

    forth = (send_a, recv_a, send_sem, recv_sem)
    back = (send_b, recv_b, back_send_sem, back_recv_sem)
    each(far_peer, 0, start, *forth)
    each(near_peer, 1, start, *forth)
    recv_a[me] = send_a[me]

    target_idx[...] = jnp.zeros_like(target_idx)
    target_idx[0:1, :] = target_ref[...].astype(jnp.float32)
    target_col = row_of(jnp.transpose(target_idx[...])[:, 0:1].astype(jnp.int32))
    pick_back[...] = as_bf16(
        lax.broadcasted_iota(jnp.int32, (elements, slots), 1) == target_col
    )
    ghost_idx[...] = jnp.full_like(ghost_idx, -1)
    for i in range(ghosts):
        ghost_idx[i : i + 1, :] = ghost_ref[i]
    ghost_cols = ghost_idx[...]
    ghost_cols = jnp.where(ghost_cols < 0, -1, row_of(ghost_cols))
    place = lax.broadcasted_iota(jnp.int32, (SUB, slots), 1)
    for b in range(beside):
        pick_ghost[b] = (place == ghost_cols[:, b : b + 1]).astype(jnp.float32)
    face_idx[...] = jnp.zeros_like(face_idx)
    listed = face_ref[...]
    shift = jnp.zeros_like(listed)
    for b in range(1, beside):
        shift = shift + (listed >= slots + b * ghosts).astype(jnp.int32) * (SUB - ghosts)
    listed = jnp.where(listed < slots, row_of(listed), listed + shift)
    face_idx[0:faces, :] = listed.astype(jnp.float32)
    face_cols = jnp.transpose(face_idx[...])
    flipped = jnp.concatenate([face_cols[half_rows:], face_cols[:half_rows]], axis=0)
    moved = (jnp.zeros_like(face_cols) + turn) > 0.5
    face_cols = jnp.where(moved, flipped, face_cols).astype(jnp.int32)
    reach = pick_face.shape[2]
    for f in range(faces):
        pick_face[f] = as_bf16(
            lax.broadcasted_iota(jnp.int32, (slots, reach), 1) == face_cols[:, f : f + 1]
        )

    spread_mode = spread_mode_ref[...]
    spread_quant = spread_quant_ref[...]

    def expand(table, spread, transposed):
        hi, lo = halves(table)
        dims = ((1,), (1,)) if transposed else ((1,), (0,))
        left = dot(spread, hi, dims) + dot(spread, lo, dims)
        hi, lo = halves(left)
        return dot(hi, spread, nt) + dot(lo, spread, nt)

    def fill(ref, column, mode_part, quant_part):
        hi, lo = halves(mode_part * quant_part)
        at = slice(column * width, (column + 1) * width)
        ref[0:width, at] = hi
        ref[width : 2 * width, at] = hi
        ref[2 * width : 3 * width, at] = lo

    for c in range(dirs):
        solver = expand(star_ref[:, c, :], spread_quant, False)
        fill(w_derive, c, expand(stiff_ref[c], spread_mode, False), -solver)
        fill(w_local, c, expand(stiff_ref[c], spread_mode, True), solver)
    for f in range(faces):
        solver = expand(solver_minus_ref[:, f, :], spread_quant, False)
        fill(w_local, dirs + f, expand(face_minus_ref[:, f, :], spread_mode, True), -solver)
        solver = expand(solver_plus_ref[:, f, :], spread_quant, False)
        fill(w_plus.at[f], 0, expand(face_plus_ref[:, f, :], spread_mode, True), -solver)

    near, far = coefficients(0.0, 1.0), coefficients(1.0, 2.0)
    fold = as_bf16(
        lax.broadcasted_iota(jnp.int32, (LANES, LANES), 0) % SUB
        == lax.broadcasted_iota(jnp.int32, (LANES, LANES), 1)
    )

    def derive(current, scale):
        wide = dot(triple(current), w_derive[...])
        total = scale[0] * wide[:, 0:width]
        for c in range(1, dirs):
            total = total + scale[c] * wide[:, c * width : (c + 1) * width]
        return total

    def part_rows(part):
        return slice(part * half_rows, (part + 1) * half_rows)

    scales, occupied, slow, starts = [None] * 2, [None] * 2, [None] * 2, [None] * 2
    recv_rows = recv_a.shape[1]
    for part in (1, 0):
        if part == 1:
            each(near_peer, 1, wait_in, *forth)
        else:
            each(far_peer, 0, wait_in, *forth)
        first_owner = far_base if part == 0 else near_base
        for j in range(half):
            row = recv_a[first_owner + j, recv_rows - 1 : recv_rows, :]
            lo = part * half_rows + j * cap
            extra_rows[lo : lo + cap, :] = jnp.where(
                own_lanes, jnp.broadcast_to(row, (cap, LANES)), 0.0
            )
        hi, mid, lo = thirds(extra_rows[part_rows(part), :])
        listed = (dot(lo, fold) + dot(mid, fold)) + dot(hi, fold)
        scales[part] = [listed[:, i : i + 1] for i in range(dirs + faces)]
        weight = listed[:, dirs + faces : dirs + faces + 1]
        occupied[part] = (weight > 0.5).astype(jnp.float32)
        slow[part] = (weight > 1.5).astype(jnp.float32)
        current = unpack(recv_a, part)
        state[part_rows(part), :] = current
        first = current * near[0]
        later = current * far[0]
        for k in range(1, ORDER):
            current = derive(current, scales[part])
            first = first + current * near[k]
            later = later + current * far[k]
        first_ref[part_rows(part), :] = first
        later_ref[part_rows(part), :] = later

    def joined(parts):
        return jnp.concatenate(parts, axis=0)

    scale_all = [joined([scales[0][i], scales[1][i]]) for i in range(dirs + faces)]
    occupied_all = joined(occupied)
    slow_all = joined(slow)

    def exchange(values, step):
        hi, lo = halves(values)
        both = jnp.concatenate([hi, lo], axis=1)
        copies = []
        for b, offset in enumerate(neighbour_steps):
            out = dot(pick_ghost[b].astype(jnp.bfloat16), both)
            ghost_send[step, b] = out[:, 0:width] + out[:, width:]
        for b, offset in enumerate(neighbour_steps):
            copy = pltpu.make_async_remote_copy(
                src_ref=ghost_send.at[step, b],
                dst_ref=ghost_recv.at[step, b],
                send_sem=ghost_send_sem.at[step, b],
                recv_sem=ghost_recv_sem.at[step, b],
                device_id=(lax.rem(me + offset + n, n),),
                device_id_type=MESH,
            )
            copy.start()
            copies.append(copy)
        return both, copies

    def own_change(both, rows, scale):
        mine_part = both[rows]
        wide = dot(jnp.concatenate([mine_part, mine_part[:, 0:width]], axis=1), w_local[...])
        change = scale[0] * wide[:, 0:width]
        for i in range(1, dirs + faces):
            change = change + scale[i] * wide[:, i * width : (i + 1) * width]
        picked = [
            dot(pick_face[f, rows, 0:slots], both).astype(jnp.bfloat16) for f in range(faces)
        ]
        return change, picked

    def ghost_table(copies, step):
        for copy in copies:
            copy.wait()
        hi, lo = halves(jnp.concatenate([ghost_recv[step, b] for b in range(beside)], axis=0))
        return jnp.concatenate([hi, lo], axis=1)

    def face_change(change, picked, table, rows, scale):
        for f in range(faces):
            both = picked[f] + dot(pick_face[f, rows, slots:reach], table).astype(jnp.bfloat16)
            both = jnp.concatenate([both, both[:, 0:width]], axis=1)
            change = change + scale[dirs + f] * dot(both, w_plus[f])
        return change

    every = slice(0, slots)
    both, copies = exchange(first_ref[...], 0)
    change, picked = own_change(both, every, scale_all)
    change = face_change(change, picked, ghost_table(copies, 0), every, scale_all)
    middle = state[...] + occupied_all * change
    state[...] = middle
    fresh = middle * near[0]
    current = middle
    for k in range(1, ORDER):
        current = derive(current, scale_all)
        fresh = fresh + current * near[k]
    second = jnp.where(slow_all > 0.5, later_ref[...], fresh)
    both, copies = exchange(second, 1)
    for part in (0, 1):
        rows = part_rows(part)
        change, picked = own_change(both, rows, scales[part])
        if part == 0:
            table = ghost_table(copies, 1)
        change = face_change(change, picked, table, rows, scales[part])
        final = state[rows, :] + occupied[part] * change
        first_owner = far_base if part == 0 else near_base
        pack(final, send_b, [first_owner + j for j in range(half)])
        if part == 0:
            each(far_peer, 0, start, *back)
        else:
            each(near_peer, 1, start, *back)
    recv_b[me] = send_b[me]
    home = None
    for part in (1, 0):
        if part == 1:
            each(near_peer, 1, wait_in, *back)
        else:
            each(far_peer, 0, wait_in, *back)
        hi, mid, lo = thirds(unpack(recv_b, part))
        table = pick_back[:, part_rows(part)]
        piece = (dot(table, lo) + dot(table, mid)) + dot(table, hi)
        home = piece if home is None else home + piece
    home = jnp.transpose(home)
    for q in range(quants):
        out_ref[q] = home[q * modes : (q + 1) * modes, :]
    for refs in (forth, back):
        each(far_peer, 0, wait_out, *refs)
        each(near_peer, 1, wait_out, *refs)


def local(
    n,
    modal_dofs,
    jacobian,
    face_area,
    cluster_id,
    target_slot,
    ghost_slots,
    face_neighbours,
    stiffness,
    star_matrix,
    face_minus,
    face_plus,
    solver_minus,
    solver_plus,
):
    modes, quants, elements = modal_dofs.shape
    flat = quants * modes
    slots = face_neighbours.shape[1]
    faces, dirs = face_area.shape[0], jacobian.shape[0]
    cap = slots // n
    beside, ghosts = ghost_slots.shape[1:]
    width = round_up(flat, LANES)
    wire_rows = (width // LANES - 1) * cap + -(-cap // 2)
    assert width - flat >= LANES // 2 and cap * SUB <= LANES
    feature = np.arange(width)
    live = feature < flat
    spread_mode = (feature[:, None] % modes == np.arange(modes)[None, :]) & live[:, None]
    spread_quant = (feature[:, None] // modes == np.arange(quants)[None, :]) & live[:, None]
    vmem = pl.BlockSpec(memory_space=pltpu.VMEM)
    f32, bf16 = jnp.float32, jnp.bfloat16
    dma = pltpu.SemaphoreType.DMA
    args = (
        jnp.transpose(modal_dofs, (1, 0, 2)),
        jacobian,
        face_area,
        cluster_id.reshape(1, elements),
        target_slot.reshape(1, elements),
        jnp.transpose(ghost_slots, (2, 0, 1)),
        face_neighbours,
        jnp.asarray(spread_mode, bf16),
        jnp.asarray(spread_quant, bf16),
        stiffness,
        jnp.transpose(star_matrix, (1, 0, 2)),
        jnp.transpose(face_minus, (1, 0, 2)),
        jnp.transpose(face_plus, (1, 0, 2)),
        jnp.transpose(solver_minus, (1, 0, 2)),
        jnp.transpose(solver_plus, (1, 0, 2)),
    )
    out = pl.pallas_call(
        functools.partial(kernel, n),
        out_shape=jax.ShapeDtypeStruct((quants, modes, elements), f32),
        in_specs=[vmem] * len(args),
        out_specs=vmem,
        scratch_shapes=[
            pltpu.VMEM((width + LANES, elements), f32),
            pltpu.VMEM((n, wire_rows + 1, LANES), f32),
            pltpu.VMEM((n, wire_rows + 1, LANES), f32),
            pltpu.VMEM((n, wire_rows, LANES), f32),
            pltpu.VMEM((n, wire_rows, LANES), f32),
            pltpu.VMEM((2, beside, SUB, width), f32),
            pltpu.VMEM((2, beside, SUB, width), f32),
            pltpu.VMEM((slots, width), f32),
            pltpu.VMEM((slots, LANES), f32),
            pltpu.VMEM((slots, width), f32),
            pltpu.VMEM((slots, width), f32),
            pltpu.VMEM((3 * width, dirs * width), bf16),
            pltpu.VMEM((3 * width, (dirs + faces) * width), bf16),
            pltpu.VMEM((faces, 3 * width, width), bf16),
            pltpu.VMEM((faces, slots, slots + beside * SUB), bf16),
            pltpu.VMEM((beside, SUB, slots), f32),
            pltpu.VMEM((elements, slots), bf16),
            pltpu.VMEM((SUB, beside), jnp.int32),
            pltpu.VMEM((SUB, slots), f32),
            pltpu.VMEM((SUB, elements), f32),
            pltpu.VMEM((SUB, elements), f32),
            dma((n,)),
            dma((n,)),
            dma((n,)),
            dma((n,)),
            dma((2, beside)),
            dma((2, beside)),
        ],
        compiler_params=pltpu.CompilerParams(
            collective_id=0, has_side_effects=True, vmem_limit_bytes=56 * 2**20
        ),
    )(*args)
    return jnp.transpose(out, (1, 0, 2))


def solution(mesh):
    placed = (
        P(None, None, "dom"),
        P(None, "dom"),
        P(None, "dom"),
        P("dom"),
        P("dom"),
        P("dom", None, None),
        P(None, "dom"),
        P(),
        P(),
        P(),
        P(),
        P(),
        P(),
    )
    return jax.shard_map(
        functools.partial(local, mesh.shape["dom"]),
        mesh=mesh,
        in_specs=placed,
        out_specs=P(None, None, "dom"),
        check_vma=False,
    )
```
